32 devices in a mesh: grp: 4 (over y, core), tm: 8 (over z, x).
Axes of the slice: x: 2, y: 2, z: 4, core: 2. Of those that a mesh axis runs over, the one named last changes fastest.
Arguments:
- wave: bfloat16 [4, 327680], P('grp', 'tm'), may hold values from -6 to 6
- assign: int32 [4, 1024], P('grp', 'tm'), may hold values from 0 to 16383
- w_first: bfloat16 [10, 512], replicated, may hold values from -2 to 2
- w_mid: bfloat16 [4, 1536, 512], replicated, may hold values from -0.15625 to 0.15625
- w_tail: bfloat16 [2, 1024, 512], replicated, may hold values from -0.1875 to 0.1875
- w_proj: bfloat16 [512, 768], replicated, may hold values from -0.25 to 0.25
- centroids: float32 [16384, 768], P('tm'), may hold values from -6 to 6
- prior: float32 [16384], P('tm'), may hold values from 1 to 16
Outputs:
- new_centroids: float32 [16384, 768], P('tm')
- new_counts: float32 [16384], P('tm')
- distortion: float32 [4, 1024], P('grp', 'tm')
The draws below stay inside these ranges and needn't reach their ends.
All inputs are finite; a program needn't handle non-finite values.
Results may differ from the reference program's by a relative error of at most 0.007.
Values may be sent and summed in bfloat16 or wider, within the bound.
A program may use at most 128 MiB of HBM per device.

```python
import math
import jax
import jax.numpy as jnp
from jax import lax

D = 768
CH = 512
K = 16384
HALO = 80
SEQS = 4
FRAMES = 1024
SAMPLES = 327680


def plant(entries, own_key, low, top_value):
    place = [jax.random.randint(jax.random.fold_in(own_key, axis), (), 0, length) for axis, length in enumerate(entries.shape)]
    main_axis = entries.shape.index(max(entries.shape))
    neighbour = place[:main_axis] + [(place[main_axis] + 1) % entries.shape[main_axis]] + place[main_axis + 1:]
    return entries.at[tuple(place)].set(low).at[tuple(neighbour)].set(top_value)


def shard_levels(rng, shape, split, smallest, high):
    def one(position, shards_of):
        steps = jax.random.uniform(jax.random.fold_in(jax.random.fold_in(rng, 6), position), (shards_of,), jnp.float32, smallest / len(split), high / len(split))
        return jnp.repeat(jnp.exp(steps), shape[position] // shards_of).reshape((-1,) + (1,) * (len(shape) - position - 1))

    loudness = one(*split[0])
    for cut in split[1:]:
        loudness = loudness * one(*cut)
    return loudness


def scatter_about(rng, extent, scale, reach, shards=(), held_as=jnp.bfloat16):
    values = scale * jax.random.normal(rng, extent, jnp.float32)
    if shards:
        values = values * shard_levels(rng, extent, shards, -0.22, 0.18)
    return jnp.clip(values, -reach, reach).astype(held_as)


def setup_inputs(seed: int = 0) -> dict:
    seeds = jax.random.split(jax.random.key(seed), 9)
    return {
        "wave": scatter_about(seeds[0], (SEQS, SAMPLES), 1.0, 6.0, ((0, 4), (1, 8))),
        "assign": plant(jax.random.randint(seeds[1], (SEQS, FRAMES), 0, K), jax.random.fold_in(seeds[1], 1), 0, K - 1).astype(jnp.int32),
        "w_first": scatter_about(seeds[2], (10, CH), 10 ** -0.5, 2.0),
        "w_mid": scatter_about(seeds[3], (4, 3 * CH, CH), (3 * CH) ** -0.5, 0.15625),
        "w_tail": scatter_about(seeds[4], (2, 2 * CH, CH), (2 * CH) ** -0.5, 0.1875),
        "w_proj": scatter_about(seeds[5], (CH, D), CH ** -0.5, 0.25),
        "centroids": scatter_about(seeds[6], (K, D), 1.0, 6.0, ((0, 8),), jnp.float32),
        "prior": jnp.clip(jnp.exp(math.log(16.0) - 2.7725887 * jax.random.uniform(seeds[7], (K,), jnp.float32) ** shard_levels(seeds[7], (K,), ((0, 8),), -0.2, 0.2)), 1.0, 16.0),
    }


EPS = 1e-05

def norm_rows(accum):
    row_mean = lax.optimization_barrier(jnp.mean(accum, axis=-1, keepdims=True))
    centred = accum - row_mean
    spread = lax.optimization_barrier(jnp.mean(centred * centred, axis=-1, keepdims=True))
    return centred * lax.rsqrt(spread + EPS)

def activate(accum):
    return jax.nn.gelu(norm_rows(accum), approximate=False).astype(jnp.bfloat16)

def first_layer(samples, w_first):
    windows = samples.reshape(-1, 5)
    accum = jnp.dot(windows[:-1], w_first[:5], preferred_element_type=jnp.float32)
    accum = accum + jnp.dot(windows[1:], w_first[5:], preferred_element_type=jnp.float32)
    return activate(accum)

def odd_layer(inputs, weight):
    channels = inputs.shape[1]
    out_len = (inputs.shape[0] - 3) // 2 + 1
    paired = jnp.concatenate([inputs, jnp.zeros((1, channels), inputs.dtype)], axis=0).reshape(out_len + 1, 2 * channels)
    accum = jnp.dot(paired[:out_len], weight[:2 * channels], preferred_element_type=jnp.float32)
    accum = accum + jnp.dot(paired[1:, :channels], weight[2 * channels:], preferred_element_type=jnp.float32)
    return activate(accum)

def even_layer(inputs, weight):
    channels = inputs.shape[1]
    paired = inputs.reshape(inputs.shape[0] // 2, 2 * channels)
    return activate(jnp.dot(paired, weight, preferred_element_type=jnp.float32))

def encode(samples, w_first, w_mid, w_tail):
    hidden = first_layer(samples, w_first)
    for layer_num in range(4):
        hidden = odd_layer(hidden, w_mid[layer_num])
    for layer_num in range(2):
        hidden = even_layer(hidden, w_tail[layer_num])
    return hidden

def project(features, w_proj):
    normed = norm_rows(features.astype(jnp.float32)).astype(jnp.bfloat16)
    return jnp.dot(normed, w_proj, preferred_element_type=jnp.float32).astype(jnp.bfloat16)

def reference(wave, assign, w_first, w_mid, w_tail, w_proj, centroids, prior):

    def one_sequence(samples):
        padded = jnp.concatenate([samples, jnp.zeros((HALO,), samples.dtype)])
        return project(encode(padded, w_first, w_mid, w_tail), w_proj)
    frames = lax.map(one_sequence, wave)
    flat_frames = frames.reshape(-1, D).astype(jnp.float32)
    labels = assign.reshape(-1)
    rounded = lax.optimization_barrier(centroids.astype(jnp.bfloat16))
    widened = rounded.astype(jnp.float32)
    centroid_sq = lax.optimization_barrier(jnp.sum(widened * widened, axis=1))
    chosen = widened[labels]
    squares = lax.optimization_barrier(jnp.sum(flat_frames * flat_frames, axis=1))
    scores = lax.optimization_barrier(jnp.sum(flat_frames * chosen, axis=1))
    distortion = ((squares - 2.0 * scores + centroid_sq[labels]) / D).reshape(SEQS, FRAMES)
    sums = jax.ops.segment_sum(flat_frames, labels, num_segments=K)
    counts = jax.ops.segment_sum(jnp.ones(labels.shape, jnp.float32), labels, num_segments=K)
    new_counts = prior + counts
    new_centroids = (prior[:, None] * centroids + sums) / new_counts[:, None]
    return (new_centroids, new_counts, distortion)
```

```python
import jax
import jax.numpy as jnp
from jax import lax
from jax.experimental import pallas as pl
from jax.experimental.pallas import tpu as pltpu
from jax.sharding import PartitionSpec as P

HALO = 80
STRIDE = 320
PHASES = 64
EPS = 1e-05
TAIL = (
    -0.9999932050704956,
    -1.151200771331787,
    -0.45877352356910706,
    -0.05340905860066414,
    0.008078922517597675,
    -0.0007687128381803632,
    3.303830453660339e-05,
)


def passed_along(value, axis, steps):
    count = lax.axis_size(axis)
    leading, last = (max(0, -steps), min(count, count - steps))
    return lax.ppermute(value, axis, [(source, source + steps) for source in range(leading, last)])


def norm_rows(accum):
    row_mean = jnp.mean(accum, axis=-1, keepdims=True)
    centred = accum - row_mean
    spread = jnp.mean(centred * centred, axis=-1, keepdims=True)
    return centred * lax.rsqrt(spread + EPS)


def gelu(value):
    size = jnp.abs(value)
    short = jnp.minimum(size, 6.0)
    power = jnp.float32(TAIL[-1])
    for coefficient in TAIL[-2::-1]:
        power = power * short + coefficient
    return jnp.maximum(value, 0.0) - size * jnp.exp2(power)


def activate(accum):
    return gelu(norm_rows(accum)).astype(jnp.bfloat16)


def dot(left, right):
    return jnp.dot(left, right, preferred_element_type=jnp.float32)


def shifted(block, following):
    rows = block.shape[0]
    wide = pltpu.roll(block.astype(jnp.float32), rows - 1, 0)
    place = lax.broadcasted_iota(jnp.int32, wide.shape, 0)
    return jnp.where(place == rows - 1, following[:1].astype(jnp.float32), wide).astype(block.dtype)


def encoder_kernel(
    windows, halo_windows, w_first, w_mid, w_tail, w_proj, frames,
    even1, odd1, even2, odd2, even3, odd3, even4, odd4, even5, odd5, held_a, held_b,
):
    rows = windows.shape[2]
    channels = w_first.shape[1]
    sub = 32

    def finish(held, even, odd, t):
        for part in range(2):
            target = (even, odd)[part]
            for piece in range(rows // sub):
                block = held[pl.ds(part * rows + piece * sub, sub), :]
                target[t, pl.ds(piece * sub, sub), :] = activate(block)

    def pipeline(pairs, product, even, odd):
        if pairs <= 2:
            for t in range(pairs):
                held = (held_a, held_b)[t % 2]
                held[...] = product(t)
                finish(held, even, odd, t)
            return
        held_a[...] = product(0)

        def body(i, carry):
            held_b[...] = product(2 * i + 1)
            finish(held_a, even, odd, 2 * i)
            held_a[...] = product(jnp.minimum(2 * i + 2, pairs - 1))
            finish(held_b, even, odd, 2 * i + 1)
            return carry

        lax.fori_loop(0, pairs // 2, body, 0)

    def window_dot(block):
        return lax.dot_general(
            block, w_first[...], (((0,), (0,)), ((), ())), preferred_element_type=jnp.float32
        )

    pipeline(
        PHASES // 2,
        lambda t: jnp.concatenate([window_dot(windows[2 * t]), window_dot(windows[2 * t + 1])], axis=0),
        even1,
        odd1,
    )
    halo = activate(window_dot(halo_windows[...])).reshape(16, 16, channels)
    layers = ((even1, odd1, even2, odd2), (even2, odd2, even3, odd3),
              (even3, odd3, even4, odd4), (even4, odd4, even5, odd5))
    phases = PHASES
    need = 15
    for layer, (even, odd, next_even, next_odd) in enumerate(layers):
        even[phases // 2] = shifted(even[0], halo[0])

        def product(t, even=even, odd=odd, layer=layer):
            first = even[pl.ds(2 * t, 2)].reshape(2 * rows, channels)
            second = odd[pl.ds(2 * t, 2)].reshape(2 * rows, channels)
            third = even[pl.ds(2 * t + 1, 2)].reshape(2 * rows, channels)
            return (
                dot(first, w_mid[layer, 0])
                + dot(second, w_mid[layer, 1])
                + dot(third, w_mid[layer, 2])
            )

        pipeline(phases // 4, product, next_even, next_odd)
        phases //= 2
        following = (need - 3) // 2 + 1
        if following > 0:
            picked = [
                jnp.concatenate([halo[2 * s + tap] for s in range(following)], axis=0) for tap in range(3)
            ]
            accum = dot(picked[0], w_mid[layer, 0]) + dot(picked[1], w_mid[layer, 1])
            accum = accum + dot(picked[2], w_mid[layer, 2])
            halo = activate(accum).reshape(following, 16, channels)
            need = following
    pair = dot(even5[...].reshape(2 * rows, channels), w_tail[0, 0])
    pair = pair + dot(odd5[...].reshape(2 * rows, channels), w_tail[0, 1])
    pair = activate(pair)
    last = dot(pair[:rows], w_tail[1, 0]) + dot(pair[rows:], w_tail[1, 1])
    features = activate(last)
    normed = norm_rows(features.astype(jnp.float32)).astype(jnp.bfloat16)
    frames[...] = dot(normed, w_proj[...]).astype(jnp.bfloat16)


def encode(samples, tail_part, w_first, w_mid, w_tail, w_proj):
    rows = samples.shape[0] // STRIDE
    channels = w_first.shape[1]
    grid = samples.reshape(rows, STRIDE)
    halo_row = jnp.concatenate([tail_part, jnp.zeros((STRIDE - HALO,), samples.dtype)])[None]
    after = jnp.concatenate([grid[1:], halo_row])[:, :HALO]
    turned = jnp.concatenate([grid, after], axis=1).T
    low = turned[:STRIDE].reshape(PHASES, 5, rows)
    high = turned[5 : STRIDE + 5].reshape(PHASES, 5, rows)
    windows = jnp.concatenate([low, high, jnp.zeros((PHASES, 6, rows), samples.dtype)], axis=1)
    fives = tail_part.reshape(16, 5).T
    halo_windows = jnp.concatenate(
        [fives, jnp.concatenate([fives[:, 1:], jnp.zeros((5, 1), samples.dtype)], axis=1),
         jnp.zeros((6, 16), samples.dtype)], axis=0)
    halo_windows = jnp.repeat(halo_windows, 16, axis=1)
    padded_first = jnp.concatenate([w_first, jnp.zeros((6, channels), w_first.dtype)])
    scratch = []
    for level in range(5):
        half = PHASES >> (level + 1)
        scratch.append(pltpu.VMEM((half + (level < 4), rows, channels), jnp.bfloat16))
        scratch.append(pltpu.VMEM((half, rows, channels), jnp.bfloat16))
    scratch += [pltpu.VMEM((2 * rows, channels), jnp.float32)] * 2
    return pl.pallas_call(
        encoder_kernel,
        out_shape=jax.ShapeDtypeStruct((rows, w_proj.shape[1]), jnp.bfloat16),
        in_specs=[pl.BlockSpec(memory_space=pltpu.VMEM)] * 6,
        out_specs=pl.BlockSpec(memory_space=pltpu.VMEM),
        scratch_shapes=scratch,
        compiler_params=pltpu.CompilerParams(vmem_limit_bytes=48 * 2**20),
        cost_estimate=pl.CostEstimate(flops=14 * 10**9, bytes_accessed=12 * 10**6, transcendentals=9 * 10**6),
        name="encoder",
    )(windows, halo_windows, padded_first, w_mid.reshape(4, 3, channels, channels),
      w_tail.reshape(2, 2, channels, channels), w_proj)


def local(wave, assign, w_first, w_mid, w_tail, w_proj, centroids, prior):
    samples = wave[0]
    tail_part = passed_along(samples[:HALO], "tm", -1)
    own_labels = assign[0]
    shard_len = centroids.shape[0]
    feat_width = centroids.shape[1]
    first_id = lax.axis_index("tm") * shard_len
    centroid_ids = first_id + jnp.arange(shard_len, dtype=jnp.int32)
    rounded = lax.optimization_barrier(centroids.astype(jnp.bfloat16))
    widened = rounded.astype(jnp.float32)
    centroid_sq = jnp.sum(widened * widened, axis=1)
    frames = encode(samples, tail_part, w_first, w_mid, w_tail, w_proj)
    accumulate_frames = lax.all_gather(frames, "tm", axis=0, tiled=True)
    labels = lax.all_gather(own_labels, "tm", axis=0, tiled=True)
    one_hot = labels[None, :] == centroid_ids[:, None]
    hot_rows = labels[:, None] == centroid_ids[None, :]
    hot_sums = jnp.dot(
        one_hot.astype(jnp.bfloat16), accumulate_frames, preferred_element_type=jnp.float32
    )
    counts = jnp.sum(one_hot.astype(jnp.float32), axis=1)
    products = jnp.einsum(
        "rd,kd->rk", accumulate_frames, rounded, preferred_element_type=jnp.float32
    )
    frame_wide = accumulate_frames.astype(jnp.float32)
    squares = jnp.sum(frame_wide * frame_wide, axis=1)
    is_owner = (labels >= first_id) & (labels < first_id + shard_len)
    picked = jnp.sum(jnp.where(hot_rows, centroid_sq[None, :] - 2.0 * products, 0.0), axis=1)
    own_term = jnp.where(is_owner, squares + picked, 0.0)
    term_sums = lax.psum_scatter(own_term, "tm", scatter_dimension=0, tiled=True)
    distortion = (term_sums / feat_width)[None, :]
    total_sums, total_counts = (
        lax.psum(hot_sums.astype(jnp.bfloat16), "grp").astype(jnp.float32),
        lax.psum(counts.astype(jnp.bfloat16), "grp").astype(jnp.float32),
    )
    new_counts = prior + total_counts
    new_centroids = (prior[:, None] * centroids + total_sums) / new_counts[:, None]
    return (new_centroids, new_counts, distortion)


def solution(mesh):
    return jax.shard_map(
        local,
        mesh=mesh,
        in_specs=(P("grp", "tm"), P("grp", "tm"), P(), P(), P(), P(), P("tm", None), P("tm")),
        out_specs=(P("tm", None), P("tm"), P("grp", "tm")),
        check_vma=False,
    )
```

```python
import jax
import jax.numpy as jnp
from jax import lax
from jax.experimental import pallas as pl
from jax.experimental.pallas import tpu as pltpu
from jax.sharding import PartitionSpec as P

HALO = 80
STRIDE = 320
PHASES = 64
EXTRA = 16
RADIX = 128
EPS = 1e-05
TAIL = (
    -0.9999932050704956,
    -1.151200771331787,
    -0.45877352356910706,
    -0.05340905860066414,
    0.008078922517597675,
    -0.0007687128381803632,
    3.303830453660339e-05,
)


def passed_along(value, axis, steps):
    count = lax.axis_size(axis)
    leading, last = (max(0, -steps), min(count, count - steps))
    return lax.ppermute(value, axis, [(source, source + steps) for source in range(leading, last)])


def norm_rows(accum):
    row_mean = jnp.mean(accum, axis=-1, keepdims=True)
    centred = accum - row_mean
    spread = jnp.mean(centred * centred, axis=-1, keepdims=True)
    return centred * lax.rsqrt(spread + EPS)


def gelu(value):
    size = jnp.abs(value)
    short = jnp.minimum(size, 6.0)
    power = jnp.float32(TAIL[-1])
    for coefficient in TAIL[-2::-1]:
        power = power * short + coefficient
    return jnp.maximum(value, 0.0) - size * jnp.exp2(power)


def activate(accum):
    return gelu(norm_rows(accum)).astype(jnp.bfloat16)


def dot(left, right):
    return jnp.dot(left, right, preferred_element_type=jnp.float32)


def shifted(block, following):
    rows = block.shape[0]
    wide = pltpu.roll(block.astype(jnp.float32), rows - 1, 0)
    place = lax.broadcasted_iota(jnp.int32, wide.shape, 0)
    return jnp.where(place == rows - 1, following[:1].astype(jnp.float32), wide).astype(block.dtype)


def encoder_kernel(
    windows, halo_windows, w_first, w_mid, w_tail, w_proj, extra, frames,
    even1, odd1, even2, odd2, even3, odd3, even4, odd4, even5, odd5, held_a, held_b,
):
    rows = windows.shape[2]
    channels = w_first.shape[1]
    sub = 32

    def finish(held, even, odd, t):
        for part in range(2):
            target = (even, odd)[part]
            for piece in range(rows // sub):
                block = held[pl.ds(part * rows + piece * sub, sub), :]
                target[t, pl.ds(piece * sub, sub), :] = activate(block)

    def pipeline(pairs, product, even, odd):
        if pairs <= 2:
            for t in range(pairs):
                held = (held_a, held_b)[t % 2]
                held[...] = product(t)
                finish(held, even, odd, t)
            return
        held_a[...] = product(0)

        def body(i, carry):
            held_b[...] = product(2 * i + 1)
            finish(held_a, even, odd, 2 * i)
            held_a[...] = product(jnp.minimum(2 * i + 2, pairs - 1))
            finish(held_b, even, odd, 2 * i + 1)
            return carry

        lax.fori_loop(0, pairs // 2, body, 0)

    def window_dot(block):
        return lax.dot_general(
            block, w_first[...], (((0,), (0,)), ((), ())), preferred_element_type=jnp.float32
        )

    pipeline(
        PHASES // 2,
        lambda t: jnp.concatenate([window_dot(windows[2 * t]), window_dot(windows[2 * t + 1])], axis=0),
        even1,
        odd1,
    )
    halo = activate(window_dot(halo_windows[...])).reshape(16, 16, channels)
    layers = ((even1, odd1, even2, odd2), (even2, odd2, even3, odd3),
              (even3, odd3, even4, odd4), (even4, odd4, even5, odd5))
    phases = PHASES
    need = 15
    for layer, (even, odd, next_even, next_odd) in enumerate(layers):
        even[phases // 2] = shifted(even[0], halo[0])

        def product(t, even=even, odd=odd, layer=layer):
            first = even[pl.ds(2 * t, 2)].reshape(2 * rows, channels)
            second = odd[pl.ds(2 * t, 2)].reshape(2 * rows, channels)
            third = even[pl.ds(2 * t + 1, 2)].reshape(2 * rows, channels)
            return (
                dot(first, w_mid[layer, 0])
                + dot(second, w_mid[layer, 1])
                + dot(third, w_mid[layer, 2])
            )

        pipeline(phases // 4, product, next_even, next_odd)
        phases //= 2
        following = (need - 3) // 2 + 1
        if following > 0:
            picked = [
                jnp.concatenate([halo[2 * s + tap] for s in range(following)], axis=0) for tap in range(3)
            ]
            accum = dot(picked[0], w_mid[layer, 0]) + dot(picked[1], w_mid[layer, 1])
            accum = accum + dot(picked[2], w_mid[layer, 2])
            halo = activate(accum).reshape(following, 16, channels)
            need = following
    pair = dot(even5[...].reshape(2 * rows, channels), w_tail[0, 0])
    pair = pair + dot(odd5[...].reshape(2 * rows, channels), w_tail[0, 1])
    pair = activate(pair)
    last = dot(pair[:rows], w_tail[1, 0]) + dot(pair[rows:], w_tail[1, 1])
    features = activate(last)
    normed = norm_rows(features.astype(jnp.float32)).astype(jnp.bfloat16)
    frames[:rows, :] = dot(normed, w_proj[...]).astype(jnp.bfloat16)
    frames[rows:, :] = extra[...]


def encode(samples, tail_part, w_first, w_mid, w_tail, w_proj, extra):
    rows = samples.shape[0] // STRIDE
    channels = w_first.shape[1]
    grid = samples.reshape(rows, STRIDE)
    halo_row = jnp.concatenate([tail_part, jnp.zeros((STRIDE - HALO,), samples.dtype)])[None]
    after = jnp.concatenate([grid[1:], halo_row])[:, :HALO]
    turned = jnp.concatenate([grid, after], axis=1).T
    low = turned[:STRIDE].reshape(PHASES, 5, rows)
    high = turned[5 : STRIDE + 5].reshape(PHASES, 5, rows)
    windows = jnp.concatenate([low, high, jnp.zeros((PHASES, 6, rows), samples.dtype)], axis=1)
    fives = tail_part.reshape(16, 5).T
    halo_windows = jnp.concatenate(
        [fives, jnp.concatenate([fives[:, 1:], jnp.zeros((5, 1), samples.dtype)], axis=1),
         jnp.zeros((6, 16), samples.dtype)], axis=0)
    halo_windows = jnp.repeat(halo_windows, 16, axis=1)
    padded_first = jnp.concatenate([w_first, jnp.zeros((6, channels), w_first.dtype)])
    scratch = []
    for level in range(5):
        half = PHASES >> (level + 1)
        scratch.append(pltpu.VMEM((half + (level < 4), rows, channels), jnp.bfloat16))
        scratch.append(pltpu.VMEM((half, rows, channels), jnp.bfloat16))
    scratch += [pltpu.VMEM((2 * rows, channels), jnp.float32)] * 2
    return pl.pallas_call(
        encoder_kernel,
        out_shape=jax.ShapeDtypeStruct((rows + EXTRA, w_proj.shape[1]), jnp.bfloat16),
        in_specs=[pl.BlockSpec(memory_space=pltpu.VMEM)] * 7,
        out_specs=pl.BlockSpec(memory_space=pltpu.VMEM),
        scratch_shapes=scratch,
        compiler_params=pltpu.CompilerParams(vmem_limit_bytes=48 * 2**20),
        cost_estimate=pl.CostEstimate(flops=14 * 10**9, bytes_accessed=12 * 10**6, transcendentals=9 * 10**6),
        name="encoder",
    )(windows, halo_windows, padded_first, w_mid.reshape(4, 3, channels, channels),
      w_tail.reshape(2, 2, channels, channels), w_proj, extra)


def remote(source, target, sent, received, device):
    return pltpu.make_async_remote_copy(
        src_ref=source, dst_ref=target, send_sem=sent, recv_sem=received,
        device_id=device, device_id_type=pl.DeviceIdType.MESH,
    )


def gather_kernel(lines, cut, block, out, own_sem, zs, zr, xs, xr, ys, yr, cs, cr):
    g, t = lax.axis_index("grp"), lax.axis_index("tm")
    h, c = lax.div(g, 2), lax.rem(g, 2)
    own, p = lax.div(t, 2), lax.rem(t, 2)
    rows = block.shape[0]
    over_p, over_h, over_c = (g, 2 * own + 1 - p), (2 * (1 - h) + c, t), (2 * h + 1 - c, t)
    above, below = own < lines - 1, own > 0
    barrier = pltpu.get_barrier_semaphore()
    for device in (over_p, over_h, over_c):
        pl.semaphore_signal(barrier, inc=1, device_id=device, device_id_type=pl.DeviceIdType.MESH)

    @pl.when(above)
    def _():
        pl.semaphore_signal(barrier, inc=1, device_id=(g, t + 2), device_id_type=pl.DeviceIdType.MESH)

    @pl.when(below)
    def _():
        pl.semaphore_signal(barrier, inc=1, device_id=(g, t - 2), device_id_type=pl.DeviceIdType.MESH)

    pl.semaphore_wait(barrier, 3 + above.astype(jnp.int32) + below.astype(jnp.int32))

    def slot(dh, dc, line, dp):
        hh = h if dh == 0 else 1 - h
        cc = c if dc == 0 else 1 - c
        pp = p if dp == 0 else 1 - p
        return out.at[2 * hh + cc, 2 * line + pp]

    def half(ref, which):
        return ref.at[pl.ds(0, cut), :] if which == 0 else ref.at[pl.ds(cut, rows - cut), :]

    def along(way, line, source=None):
        target = slot(0, 0, line, 0)
        return remote(target if source is None else source, target, zs.at[way, line], zr.at[line],
                      (g, t + 2 - 4 * way))

    def to_p(kind, line, source=None):
        target = slot(0, 0, line, 0) if kind == 0 else half(slot(1, 0, line, 0), 1)
        return remote(target if source is None else source, target, xs.at[kind, line], xr.at[kind, line], over_p)

    def to_h(kind, line, source=None):
        target = slot(0, 0, line, 0) if kind == 0 else half(slot(0, 0, line, 1), 0)
        return remote(target if source is None else source, target, ys.at[kind, line], yr.at[kind, line], over_h)

    def to_c(dh, dp, line, source=None):
        target = slot(dh, 0, line, dp)
        kind = 2 * dh + dp
        return remote(target if source is None else source, target, cs.at[kind, line], cr.at[kind, line], over_c)

    def arrived(target, sent, received):
        remote(target, target, sent, received, over_c).wait_recv()

    here = pltpu.make_async_copy(block, slot(0, 0, own, 0), own_sem)
    onward = (above, below)

    def spread(line, source=None):
        to_p(0, line, source).start()
        to_h(0, line, source).start()
        to_c(0, 0, line, source).start()

    for way in range(2):
        @pl.when(onward[way])
        def _(way=way):
            along(way, own, block).start()
    spread(own, block)
    here.start()

    def each(step, action):
        if step == 0:
            action(own, 0)
            return
        for way in range(2):
            line = own - step if way == 0 else own + step

            @pl.when((line >= 0) & (line < lines))
            def _(line=line, way=way):
                action(line, way)

    def first_visit(line, way):
        arrived(slot(0, 0, line, 0), zs.at[way, line], zr.at[line])

        @pl.when(onward[way])
        def _():
            along(way, line).start()

        spread(line)

    def second_visit(line, way):
        arrived(slot(0, 0, line, 1), xs.at[0, line], xr.at[0, line])
        to_h(1, line).start()
        to_c(0, 1, line).start()
        arrived(slot(1, 0, line, 0), ys.at[0, line], yr.at[0, line])
        to_p(1, line).start()
        to_c(1, 0, line).start()

    def third_visit(line, way):
        arrived(half(slot(1, 0, line, 1), 0), ys.at[1, line], yr.at[1, line])
        arrived(half(slot(1, 0, line, 1), 1), xs.at[1, line], xr.at[1, line])
        to_c(1, 1, line).start()

    for step in range(1, lines):
        each(step, first_visit)
        each(step - 1, second_visit)
    each(lines - 1, second_visit)
    for step in range(lines):
        each(step, third_visit)

    def last_visit(line, way):
        for dh in range(2):
            for dp in range(2):
                kind = 2 * dh + dp
                arrived(slot(dh, 1, line, dp), cs.at[kind, line], cr.at[kind, line])
                to_c(dh, dp, line).wait_send()
        for kind in range(2):
            to_p(kind, line).wait_send()
            to_h(kind, line).wait_send()

    for step in range(lines):
        each(step, last_visit)
    for step in range(1, lines):
        def sent_on(line, way):
            @pl.when(onward[way])
            def _():
                along(way, line).wait_send()

        each(step, sent_on)
    for way in range(2):
        @pl.when(onward[way])
        def _(way=way):
            along(way, own).wait_send()
    here.wait()


def gather_blocks(block, groups, count):
    lines = count // 2
    dma = pltpu.SemaphoreType.DMA
    return pl.pallas_call(
        lambda *refs: gather_kernel(lines, 64, *refs),
        out_shape=jax.ShapeDtypeStruct((groups, count) + block.shape, block.dtype),
        in_specs=[pl.BlockSpec(memory_space=pltpu.VMEM)],
        out_specs=pl.BlockSpec(memory_space=pl.ANY),
        scratch_shapes=[dma, dma((2, lines)), dma((lines,)), dma((2, lines)), dma((2, lines)),
                        dma((2, lines)), dma((2, lines)), dma((4, lines)), dma((4, lines))],
        compiler_params=pltpu.CompilerParams(collective_id=0, has_side_effects=True, vmem_limit_bytes=4 * 2**20),
        name="gather_blocks",
    )(block)


def exchange_kernel(count, terms, out, landed, sent, received):
    g, t = lax.axis_index("grp"), lax.axis_index("tm")
    barrier = pltpu.get_barrier_semaphore()
    for step in range(1, count):
        peer = lax.rem(t + step, count)
        pl.semaphore_signal(barrier, inc=1, device_id=(g, peer), device_id_type=pl.DeviceIdType.MESH)
    pl.semaphore_wait(barrier, count - 1)
    copies = []
    for step in range(1, count):
        peer = lax.rem(t + step, count)
        copy = remote(terms.at[peer], landed.at[step - 1], sent.at[step - 1], received.at[step - 1], (g, peer))
        copy.start()
        copies.append(copy)
    total = terms[t]
    for step in range(1, count):
        copies[step - 1].wait()
        total = total + landed[step - 1]
    out[...] = total


def exchange_terms(terms):
    count, rows = terms.shape
    dma = pltpu.SemaphoreType.DMA
    return pl.pallas_call(
        lambda *refs: exchange_kernel(count, *refs),
        out_shape=jax.ShapeDtypeStruct((1, rows), terms.dtype),
        in_specs=[pl.BlockSpec(memory_space=pltpu.VMEM)],
        out_specs=pl.BlockSpec(memory_space=pltpu.VMEM),
        scratch_shapes=[pltpu.VMEM((count - 1, 1, rows), terms.dtype), dma((count - 1,)), dma((count - 1,))],
        compiler_params=pltpu.CompilerParams(collective_id=1, has_side_effects=True),
        name="exchange_terms",
    )(terms.reshape(count, 1, rows))


def local(wave, assign, w_first, w_mid, w_tail, w_proj, centroids, prior):
    samples = wave[0]
    tail_part = passed_along(samples[:HALO], "tm", -1)
    groups, count = lax.axis_size("grp"), lax.axis_size("tm")
    own_rows = assign.shape[1]
    shard_len, feat_width = centroids.shape
    digits = jnp.concatenate([assign // RADIX, assign % RADIX]).astype(jnp.bfloat16)
    extra = jnp.pad(digits, ((0, EXTRA - 2), (0, feat_width - own_rows)))
    block = encode(samples, tail_part, w_first, w_mid, w_tail, w_proj, extra)
    gathered = gather_blocks(block, groups, count)
    digits = gathered[:, :, own_rows : own_rows + 2, :own_rows].astype(jnp.int32)
    labels = digits[:, :, 0] * RADIX + digits[:, :, 1]
    labels = jnp.pad(labels, ((0, 0), (0, 0), (0, EXTRA)), constant_values=-1)
    first_id = lax.axis_index("tm") * shard_len
    centroid_ids = first_id + jnp.arange(shard_len, dtype=jnp.int32)
    rounded = lax.optimization_barrier(centroids.astype(jnp.bfloat16))
    widened = rounded.astype(jnp.float32)
    centroid_sq = jnp.sum(widened * widened, axis=1)
    one_hot = labels.reshape(1, -1) == centroid_ids[:, None]
    total_sums = jnp.dot(
        one_hot.astype(jnp.bfloat16), gathered.reshape(-1, feat_width), preferred_element_type=jnp.float32
    )
    total_counts = jnp.sum(one_hot.astype(jnp.float32), axis=1)
    group = lax.axis_index("grp")
    sequence = lax.dynamic_index_in_dim(gathered, group, 0, keepdims=False).reshape(-1, feat_width)
    own_labels = lax.dynamic_index_in_dim(labels, group, 0, keepdims=False).reshape(-1)
    hot_rows = own_labels[:, None] == centroid_ids[None, :]
    products = jnp.einsum("rd,kd->rk", sequence, rounded, preferred_element_type=jnp.float32)
    frame_wide = sequence.astype(jnp.float32)
    squares = jnp.sum(frame_wide * frame_wide, axis=1)
    is_owner = (own_labels >= first_id) & (own_labels < first_id + shard_len)
    picked = jnp.sum(jnp.where(hot_rows, centroid_sq[None, :] - 2.0 * products, 0.0), axis=1)
    own_term = jnp.where(is_owner, squares + picked, 0.0)
    term_sums = exchange_terms(own_term.reshape(count, -1)[:, :own_rows])
    distortion = term_sums / feat_width
    new_counts = prior + total_counts
    new_centroids = (prior[:, None] * centroids + total_sums) / new_counts[:, None]
    return (new_centroids, new_counts, distortion)


def solution(mesh):
    return jax.shard_map(
        local,
        mesh=mesh,
        in_specs=(P("grp", "tm"), P("grp", "tm"), P(), P(), P(), P(), P("tm", None), P("tm")),
        out_specs=(P("tm", None), P("tm"), P("grp", "tm")),
        check_vma=False,
    )
```

```python
import jax
import jax.numpy as jnp
from jax import lax
from jax.experimental import pallas as pl
from jax.experimental.pallas import tpu as pltpu
from jax.sharding import PartitionSpec as P

HALO = 80
STRIDE = 320
PHASES = 64
EXTRA = 16
RADIX = 128
EPS = 1e-05
TAIL = (
    -0.9999932050704956,
    -1.151200771331787,
    -0.45877352356910706,
    -0.05340905860066414,
    0.008078922517597675,
    -0.0007687128381803632,
    3.303830453660339e-05,
)


def passed_along(value, axis, steps):
    count = lax.axis_size(axis)
    leading, last = (max(0, -steps), min(count, count - steps))
    return lax.ppermute(value, axis, [(source, source + steps) for source in range(leading, last)])


def norm_rows(accum):
    row_mean = jnp.mean(accum, axis=-1, keepdims=True)
    centred = accum - row_mean
    spread = jnp.mean(centred * centred, axis=-1, keepdims=True)
    return centred * lax.rsqrt(spread + EPS)


def gelu(value):
    size = jnp.abs(value)
    short = jnp.minimum(size, 6.0)
    power = jnp.float32(TAIL[-1])
    for coefficient in TAIL[-2::-1]:
        power = power * short + coefficient
    return jnp.maximum(value, 0.0) - size * jnp.exp2(power)


def activate(accum):
    return gelu(norm_rows(accum)).astype(jnp.bfloat16)


def dot(left, right):
    return jnp.dot(left, right, preferred_element_type=jnp.float32)


def shifted(block, following):
    rows = block.shape[0]
    wide = pltpu.roll(block.astype(jnp.float32), rows - 1, 0)
    place = lax.broadcasted_iota(jnp.int32, wide.shape, 0)
    return jnp.where(place == rows - 1, following[:1].astype(jnp.float32), wide).astype(block.dtype)


def encoder_kernel(
    windows, halo_windows, w_first, w_mid, w_tail, w_proj, extra, frames,
    even1, odd1, even2, odd2, even3, odd3, even4, odd4, even5, odd5, held_a, held_b,
):
    rows = windows.shape[2]
    channels = w_first.shape[1]
    sub = 32

    def finish(held, even, odd, t):
        for part in range(2):
            target = (even, odd)[part]
            for piece in range(rows // sub):
                block = held[pl.ds(part * rows + piece * sub, sub), :]
                target[t, pl.ds(piece * sub, sub), :] = activate(block)

    def pipeline(pairs, product, even, odd):
        if pairs <= 2:
            for t in range(pairs):
                held = (held_a, held_b)[t % 2]
                held[...] = product(t)
                finish(held, even, odd, t)
            return
        held_a[...] = product(0)

        def body(i, carry):
            held_b[...] = product(2 * i + 1)
            finish(held_a, even, odd, 2 * i)
            held_a[...] = product(jnp.minimum(2 * i + 2, pairs - 1))
            finish(held_b, even, odd, 2 * i + 1)
            return carry

        lax.fori_loop(0, pairs // 2, body, 0)

    def window_dot(block):
        return lax.dot_general(
            block, w_first[...], (((0,), (0,)), ((), ())), preferred_element_type=jnp.float32
        )

    pipeline(
        PHASES // 2,
        lambda t: jnp.concatenate([window_dot(windows[2 * t]), window_dot(windows[2 * t + 1])], axis=0),
        even1,
        odd1,
    )
    halo = activate(window_dot(halo_windows[...])).reshape(16, 16, channels)
    layers = ((even1, odd1, even2, odd2), (even2, odd2, even3, odd3),
              (even3, odd3, even4, odd4), (even4, odd4, even5, odd5))
    phases = PHASES
    need = 15
    for layer, (even, odd, next_even, next_odd) in enumerate(layers):
        even[phases // 2] = shifted(even[0], halo[0])

        def product(t, even=even, odd=odd, layer=layer):
            first = even[pl.ds(2 * t, 2)].reshape(2 * rows, channels)
            second = odd[pl.ds(2 * t, 2)].reshape(2 * rows, channels)
            third = even[pl.ds(2 * t + 1, 2)].reshape(2 * rows, channels)
            return (
                dot(first, w_mid[layer, 0])
                + dot(second, w_mid[layer, 1])
                + dot(third, w_mid[layer, 2])
            )

        pipeline(phases // 4, product, next_even, next_odd)
        phases //= 2
        following = (need - 3) // 2 + 1
        if following > 0:
            picked = [
                jnp.concatenate([halo[2 * s + tap] for s in range(following)], axis=0) for tap in range(3)
            ]
            accum = dot(picked[0], w_mid[layer, 0]) + dot(picked[1], w_mid[layer, 1])
            accum = accum + dot(picked[2], w_mid[layer, 2])
            halo = activate(accum).reshape(following, 16, channels)
            need = following
    pair = dot(even5[...].reshape(2 * rows, channels), w_tail[0, 0])
    pair = pair + dot(odd5[...].reshape(2 * rows, channels), w_tail[0, 1])
    pair = activate(pair)
    last = dot(pair[:rows], w_tail[1, 0]) + dot(pair[rows:], w_tail[1, 1])
    features = activate(last)
    normed = norm_rows(features.astype(jnp.float32)).astype(jnp.bfloat16)
    frames[:rows, :] = dot(normed, w_proj[...]).astype(jnp.bfloat16)
    frames[rows:, :] = extra[...]


def encode(samples, tail_part, w_first, w_mid, w_tail, w_proj, extra):
    rows = samples.shape[0] // STRIDE
    channels = w_first.shape[1]
    grid = samples.reshape(rows, STRIDE)
    halo_row = jnp.concatenate([tail_part, jnp.zeros((STRIDE - HALO,), samples.dtype)])[None]
    after = jnp.concatenate([grid[1:], halo_row])[:, :HALO]
    turned = jnp.concatenate([grid, after], axis=1).T
    low = turned[:STRIDE].reshape(PHASES, 5, rows)
    high = turned[5 : STRIDE + 5].reshape(PHASES, 5, rows)
    windows = jnp.concatenate([low, high, jnp.zeros((PHASES, 6, rows), samples.dtype)], axis=1)
    fives = tail_part.reshape(16, 5).T
    halo_windows = jnp.concatenate(
        [fives, jnp.concatenate([fives[:, 1:], jnp.zeros((5, 1), samples.dtype)], axis=1),
         jnp.zeros((6, 16), samples.dtype)], axis=0)
    halo_windows = jnp.repeat(halo_windows, 16, axis=1)
    padded_first = jnp.concatenate([w_first, jnp.zeros((6, channels), w_first.dtype)])
    scratch = []
    for level in range(5):
        half = PHASES >> (level + 1)
        scratch.append(pltpu.VMEM((half + (level < 4), rows, channels), jnp.bfloat16))
        scratch.append(pltpu.VMEM((half, rows, channels), jnp.bfloat16))
    scratch += [pltpu.VMEM((2 * rows, channels), jnp.float32)] * 2
    return pl.pallas_call(
        encoder_kernel,
        out_shape=jax.ShapeDtypeStruct((rows + EXTRA, w_proj.shape[1]), jnp.bfloat16),
        in_specs=[pl.BlockSpec(memory_space=pltpu.VMEM)] * 7,
        out_specs=pl.BlockSpec(memory_space=pltpu.VMEM),
        scratch_shapes=scratch,
        compiler_params=pltpu.CompilerParams(vmem_limit_bytes=48 * 2**20),
        cost_estimate=pl.CostEstimate(flops=14 * 10**9, bytes_accessed=12 * 10**6, transcendentals=9 * 10**6),
        name="encoder",
    )(windows, halo_windows, padded_first, w_mid.reshape(4, 3, channels, channels),
      w_tail.reshape(2, 2, channels, channels), w_proj, extra)


def remote(source, target, sent, received, device):
    return pltpu.make_async_remote_copy(
        src_ref=source, dst_ref=target, send_sem=sent, recv_sem=received,
        device_id=device, device_id_type=pl.DeviceIdType.MESH,
    )


def gather_kernel(
    lines, cut, block, centroids, sums, counts, term, out, rounded, squares, terms, landed,
    own_sem, zs, zr, xs, xr, ys, yr, cs, cr, ts, tr,
):
    g, t = lax.axis_index("grp"), lax.axis_index("tm")
    h, c = lax.div(g, 2), lax.rem(g, 2)
    own, p = lax.div(t, 2), lax.rem(t, 2)
    rows = block.shape[0]
    over_p, over_h, over_c = (g, 2 * own + 1 - p), (2 * (1 - h) + c, t), (2 * h + 1 - c, t)
    above, below = own < lines - 1, own > 0
    barrier = pltpu.get_barrier_semaphore()
    devices = 2 * lines
    peers = [(g, lax.rem(t + step, devices)) for step in range(1, devices)]
    for device in peers + [over_h, over_c]:
        pl.semaphore_signal(barrier, inc=1, device_id=device, device_id_type=pl.DeviceIdType.MESH)
    pl.semaphore_wait(barrier, devices + 1)

    def slot(dh, dc, line, dp):
        hh = h if dh == 0 else 1 - h
        cc = c if dc == 0 else 1 - c
        pp = p if dp == 0 else 1 - p
        return out.at[2 * hh + cc, 2 * line + pp]

    def half(ref, which):
        return ref.at[pl.ds(0, cut), :] if which == 0 else ref.at[pl.ds(cut, rows - cut), :]

    def along(way, line, source=None):
        target = slot(0, 0, line, 0)
        return remote(target if source is None else source, target, zs.at[way, line], zr.at[line],
                      (g, t + 2 - 4 * way))

    def to_p(kind, line, source=None):
        target = slot(0, 0, line, 0) if kind == 0 else half(slot(1, 0, line, 0), 1)
        return remote(target if source is None else source, target, xs.at[kind, line], xr.at[kind, line], over_p)

    def to_h(kind, line, source=None):
        target = slot(0, 0, line, 0) if kind == 0 else half(slot(0, 0, line, 1), 0)
        return remote(target if source is None else source, target, ys.at[kind, line], yr.at[kind, line], over_h)

    def to_c(dh, dp, line, source=None):
        target = slot(dh, 0, line, dp)
        kind = 2 * dh + dp
        return remote(target if source is None else source, target, cs.at[kind, line], cr.at[kind, line], over_c)

    def arrived(target, sent, received):
        remote(target, target, sent, received, over_c).wait_recv()

    here = pltpu.make_async_copy(block, slot(0, 0, own, 0), own_sem)
    onward = (above, below)

    def spread(line, source=None):
        to_p(0, line, source).start()
        to_h(0, line, source).start()
        to_c(0, 0, line, source).start()

    for way in range(2):
        @pl.when(onward[way])
        def _(way=way):
            along(way, own, block).start()
    spread(own, block)
    here.start()

    def each(step, action):
        if step == 0:
            action(own, 0)
            return
        for way in range(2):
            line = own - step if way == 0 else own + step

            @pl.when((line >= 0) & (line < lines))
            def _(line=line, way=way):
                action(line, way)

    def first_visit(line, way):
        arrived(slot(0, 0, line, 0), zs.at[way, line], zr.at[line])

        @pl.when(onward[way])
        def _():
            along(way, line).start()

        spread(line)

    def second_visit(line, way):
        arrived(slot(0, 0, line, 1), xs.at[0, line], xr.at[0, line])
        to_h(1, line).start()
        to_c(0, 1, line).start()
        arrived(slot(1, 0, line, 0), ys.at[0, line], yr.at[0, line])
        to_p(1, line).start()
        to_c(1, 0, line).start()

    def third_visit(line, way):
        arrived(half(slot(1, 0, line, 1), 0), ys.at[1, line], yr.at[1, line])
        arrived(half(slot(1, 0, line, 1), 1), xs.at[1, line], xr.at[1, line])
        to_c(1, 1, line).start()

    shard, width = centroids.shape
    frame_rows = counts.shape[1]
    tile = 256
    first_id = t * shard

    def prepare(i, carry):
        held = pl.ds(pl.multiple_of(i * tile, tile), tile)
        short = centroids[held, :].astype(jnp.bfloat16)
        rounded[held, :] = short
        wide = short.astype(jnp.float32)
        squares[held, :] = jnp.broadcast_to(jnp.sum(wide * wide, axis=1, keepdims=True), (tile, frame_rows))
        sums[held, :] = jnp.zeros((tile, width), jnp.float32)
        counts[held, :] = jnp.zeros((tile, frame_rows), jnp.float32)
        return carry

    lax.fori_loop(0, shard // tile, prepare, 0)

    def accumulate(dh, dc, line, scored):
        group = 2 * (h if dh == 0 else 1 - h) + (c if dc == 0 else 1 - c)
        pair = [out[group, 2 * line + k, pl.ds(0, frame_rows), :] for k in range(2)]
        pair = jnp.concatenate(pair, axis=0)
        labels = []
        for k in range(2):
            digits = out[group, 2 * line + k, pl.ds(frame_rows, EXTRA), pl.ds(0, frame_rows)].astype(jnp.float32)
            labels.append(digits[0:1] * float(RADIX) + digits[1:2])
        labels = jnp.concatenate(labels, axis=1)

        def one(i, picked):
            held = pl.ds(pl.multiple_of(i * tile, tile), tile)
            ids = lax.broadcasted_iota(jnp.int32, (tile, 2 * frame_rows), 0) + (first_id + i * tile)
            hot = ids.astype(jnp.float32) == labels
            ones = jnp.where(hot, 1.0, 0.0)
            sums[held, :] += dot(ones.astype(jnp.bfloat16), pair)
            counts[held, :] += ones[:, :frame_rows] + ones[:, frame_rows:]
            if not scored:
                return picked
            products = lax.dot_general(
                rounded[held, :], pair, (((1,), (1,)), ((), ())), preferred_element_type=jnp.float32
            )
            value = jnp.where(hot, squares[held, :][:, :1] - 2.0 * products, 0.0)
            return picked + jnp.sum(value, axis=0, keepdims=True)

        picked = lax.fori_loop(0, shard // tile, one, jnp.zeros((1, 2 * frame_rows), jnp.float32))
        if scored:
            terms[2 * line] = picked[:, :frame_rows]
            terms[2 * line + 1] = picked[:, frame_rows:]

    def each_rolled(step, action):
        if step < 0 or step >= lines:
            return
        if step == 0:
            action(own)
            return

        def body(way, carry):
            line = own - step + 2 * step * way

            @pl.when((line >= 0) & (line < lines))
            def _():
                action(line)

            return carry

        lax.fori_loop(0, 2, body, 0)

    def to_peer(peer):
        return remote(terms.at[peer], landed.at[t], ts.at[peer], tr.at[t], (g, peer))

    def compute_0(line):
        accumulate(0, 0, line, True)

    def compute_1(line):
        for dp in range(2):
            arrived(slot(0, 1, line, dp), cs.at[dp, line], cr.at[dp, line])
        for k in range(2):
            @pl.when(2 * line + k != t)
            def _(k=k):
                to_peer(2 * line + k).start()

        accumulate(0, 1, line, False)

    def compute_2(line):
        accumulate(1, 0, line, False)

    def compute_3(line):
        for dp in range(2):
            arrived(slot(1, 1, line, dp), cs.at[2 + dp, line], cr.at[2 + dp, line])
        accumulate(1, 1, line, False)

    for step in range(1, lines):
        each(step, first_visit)
        each(step - 1, second_visit)
        if step == 1:
            here.wait()
        each_rolled(step - 1, compute_0)
        each_rolled(step - 2, compute_1)
    each(lines - 1, second_visit)
    each_rolled(lines - 1, compute_0)
    each(0, third_visit)
    each_rolled(lines - 2, compute_1)
    for step in range(lines):
        if step + 1 < lines:
            each(step + 1, third_visit)
        each_rolled(step, compute_2)
        if step == 0:
            each_rolled(lines - 1, compute_1)
        each_rolled(step - 1, compute_3)
    each_rolled(lines - 1, compute_3)

    def last_visit(line, way):
        for dh in range(2):
            for dp in range(2):
                kind = 2 * dh + dp
                to_c(dh, dp, line).wait_send()
        for kind in range(2):
            to_p(kind, line).wait_send()
            to_h(kind, line).wait_send()

    for step in range(lines):
        each(step, last_visit)
    for step in range(1, lines):
        def sent_on(line, way):
            @pl.when(onward[way])
            def _():
                along(way, line).wait_send()

        each(step, sent_on)
    for way in range(2):
        @pl.when(onward[way])
        def _(way=way):
            along(way, own).wait_send()
    landed[t] = terms[t]

    def settle(peer, carry):
        @pl.when(peer != t)
        def _():
            to_peer(peer).wait_send()
            arrived_term = remote(landed.at[peer], landed.at[peer], ts.at[peer], tr.at[peer], over_c)
            arrived_term.wait_recv()

        return carry

    lax.fori_loop(0, devices, settle, 0)
    total = landed[0]
    for peer in range(1, devices):
        total = total + landed[peer]
    term[...] = total


def gather_and_sum(block, centroids, groups, count, frame_rows):
    lines = count // 2
    shard, width = centroids.shape
    dma = pltpu.SemaphoreType.DMA
    vmem = pl.BlockSpec(memory_space=pltpu.VMEM)
    return pl.pallas_call(
        lambda *refs: gather_kernel(lines, 64, *refs),
        out_shape=(
            jax.ShapeDtypeStruct((shard, width), jnp.float32),
            jax.ShapeDtypeStruct((shard, frame_rows), jnp.float32),
            jax.ShapeDtypeStruct((1, frame_rows), jnp.float32),
        ),
        in_specs=[vmem, vmem],
        out_specs=(vmem, vmem, vmem),
        scratch_shapes=[
            pltpu.VMEM((groups, count) + block.shape, block.dtype),
            pltpu.VMEM((shard, width), jnp.bfloat16),
            pltpu.VMEM((shard, frame_rows), jnp.float32),
            pltpu.VMEM((count, 1, frame_rows), jnp.float32),
            pltpu.VMEM((count, 1, frame_rows), jnp.float32),
            dma, dma((2, lines)), dma((lines,)), dma((2, lines)), dma((2, lines)),
            dma((2, lines)), dma((2, lines)), dma((4, lines)), dma((4, lines)),
            dma((count,)), dma((count,)),
        ],
        compiler_params=pltpu.CompilerParams(collective_id=0, has_side_effects=True, vmem_limit_bytes=50 * 2**20),
        name="gather_and_sum",
    )(block, centroids)


def local(wave, assign, w_first, w_mid, w_tail, w_proj, centroids, prior):
    samples = wave[0]
    tail_part = passed_along(samples[:HALO], "tm", -1)
    groups, count = lax.axis_size("grp"), lax.axis_size("tm")
    own_rows = assign.shape[1]
    feat_width = centroids.shape[1]
    digits = jnp.concatenate([assign // RADIX, assign % RADIX]).astype(jnp.bfloat16)
    extra = jnp.pad(digits, ((0, EXTRA - 2), (0, feat_width - own_rows)))
    block = encode(samples, tail_part, w_first, w_mid, w_tail, w_proj, extra)
    total_sums, lane_counts, term = gather_and_sum(block, centroids, groups, count, own_rows)
    own_frames = block[:own_rows].astype(jnp.float32)
    squares = jnp.sum(own_frames * own_frames, axis=1)
    distortion = (squares[None, :] + term) / feat_width
    total_counts = jnp.sum(lane_counts, axis=1)
    new_counts = prior + total_counts
    new_centroids = (prior[:, None] * centroids + total_sums) / new_counts[:, None]
    return (new_centroids, new_counts, distortion)


def solution(mesh):
    return jax.shard_map(
        local,
        mesh=mesh,
        in_specs=(P("grp", "tm"), P("grp", "tm"), P(), P(), P(), P(), P("tm", None), P("tm")),
        out_specs=(P("tm", None), P("tm"), P("grp", "tm")),
        check_vma=False,
    )
```

```python
import jax
import jax.numpy as jnp
from jax import lax
from jax.experimental import pallas as pl
from jax.experimental.pallas import tpu as pltpu
from jax.sharding import PartitionSpec as P

HALO = 80
STRIDE = 320
PHASES = 64
EXTRA = 16
RADIX = 128
EPS = 1e-05
TAIL = (
    -0.9999932050704956,
    -1.151200771331787,
    -0.45877352356910706,
    -0.05340905860066414,
    0.008078922517597675,
    -0.0007687128381803632,
    3.303830453660339e-05,
)


def passed_along(value, axis, steps):
    count = lax.axis_size(axis)
    leading, last = (max(0, -steps), min(count, count - steps))
    return lax.ppermute(value, axis, [(source, source + steps) for source in range(leading, last)])


def norm_rows(accum):
    row_mean = jnp.mean(accum, axis=-1, keepdims=True)
    centred = accum - row_mean
    spread = jnp.mean(centred * centred, axis=-1, keepdims=True)
    return centred * lax.rsqrt(spread + EPS)


def gelu(value):
    size = jnp.abs(value)
    short = jnp.minimum(size, 6.0)
    power = jnp.float32(TAIL[-1])
    for coefficient in TAIL[-2::-1]:
        power = power * short + coefficient
    return jnp.maximum(value, 0.0) - size * jnp.exp2(power)


def activate(accum):
    return gelu(norm_rows(accum)).astype(jnp.bfloat16)


def dot(left, right):
    return jnp.dot(left, right, preferred_element_type=jnp.float32)


def shifted(block, following):
    rows = block.shape[0]
    wide = pltpu.roll(block.astype(jnp.float32), rows - 1, 0)
    place = lax.broadcasted_iota(jnp.int32, wide.shape, 0)
    return jnp.where(place == rows - 1, following[:1].astype(jnp.float32), wide).astype(block.dtype)


def encoder_kernel(
    windows, halo_windows, w_first, w_mid, w_tail, w_proj, extra, frames,
    even1, odd1, even2, odd2, even3, odd3, even4, odd4, even5, odd5, held_a, held_b,
):
    rows = windows.shape[2]
    channels = w_first.shape[1]
    sub = 32

    def finish(held, even, odd, t):
        for part in range(2):
            target = (even, odd)[part]
            for piece in range(rows // sub):
                block = held[pl.ds(part * rows + piece * sub, sub), :]
                target[t, pl.ds(piece * sub, sub), :] = activate(block)

    def pipeline(pairs, product, even, odd):
        if pairs <= 2:
            for t in range(pairs):
                held = (held_a, held_b)[t % 2]
                held[...] = product(t)
                finish(held, even, odd, t)
            return
        held_a[...] = product(0)

        def body(i, carry):
            held_b[...] = product(2 * i + 1)
            finish(held_a, even, odd, 2 * i)
            held_a[...] = product(jnp.minimum(2 * i + 2, pairs - 1))
            finish(held_b, even, odd, 2 * i + 1)
            return carry

        lax.fori_loop(0, pairs // 2, body, 0)

    def window_dot(block):
        return lax.dot_general(
            block, w_first[...], (((0,), (0,)), ((), ())), preferred_element_type=jnp.float32
        )

    pipeline(
        PHASES // 2,
        lambda t: jnp.concatenate([window_dot(windows[2 * t]), window_dot(windows[2 * t + 1])], axis=0),
        even1,
        odd1,
    )
    halo = activate(window_dot(halo_windows[...])).reshape(16, 16, channels)
    layers = ((even1, odd1, even2, odd2), (even2, odd2, even3, odd3),
              (even3, odd3, even4, odd4), (even4, odd4, even5, odd5))
    phases = PHASES
    need = 15
    for layer, (even, odd, next_even, next_odd) in enumerate(layers):
        even[phases // 2] = shifted(even[0], halo[0])

        def product(t, even=even, odd=odd, layer=layer):
            first = even[pl.ds(2 * t, 2)].reshape(2 * rows, channels)
            second = odd[pl.ds(2 * t, 2)].reshape(2 * rows, channels)
            third = even[pl.ds(2 * t + 1, 2)].reshape(2 * rows, channels)
            return (
                dot(first, w_mid[layer, 0])
                + dot(second, w_mid[layer, 1])
                + dot(third, w_mid[layer, 2])
            )

        pipeline(phases // 4, product, next_even, next_odd)
        phases //= 2
        following = (need - 3) // 2 + 1
        if following > 0:
            picked = [
                jnp.concatenate([halo[2 * s + tap] for s in range(following)], axis=0) for tap in range(3)
            ]
            accum = dot(picked[0], w_mid[layer, 0]) + dot(picked[1], w_mid[layer, 1])
            accum = accum + dot(picked[2], w_mid[layer, 2])
            halo = activate(accum).reshape(following, 16, channels)
            need = following
    pair = dot(even5[...].reshape(2 * rows, channels), w_tail[0, 0])
    pair = pair + dot(odd5[...].reshape(2 * rows, channels), w_tail[0, 1])
    pair = activate(pair)
    last = dot(pair[:rows], w_tail[1, 0]) + dot(pair[rows:], w_tail[1, 1])
    features = activate(last)
    normed = norm_rows(features.astype(jnp.float32)).astype(jnp.bfloat16)
    frames[:rows, :] = dot(normed, w_proj[...]).astype(jnp.bfloat16)
    frames[rows:, :] = extra[...]


def encode(samples, tail_part, w_first, w_mid, w_tail, w_proj, extra):
    rows = samples.shape[0] // STRIDE
    channels = w_first.shape[1]
    grid = samples.reshape(rows, STRIDE)
    halo_row = jnp.concatenate([tail_part, jnp.zeros((STRIDE - HALO,), samples.dtype)])[None]
    after = jnp.concatenate([grid[1:], halo_row])[:, :HALO]
    turned = jnp.concatenate([grid, after], axis=1).T
    low = turned[:STRIDE].reshape(PHASES, 5, rows)
    high = turned[5 : STRIDE + 5].reshape(PHASES, 5, rows)
    windows = jnp.concatenate([low, high, jnp.zeros((PHASES, 6, rows), samples.dtype)], axis=1)
    fives = tail_part.reshape(16, 5).T
    halo_windows = jnp.concatenate(
        [fives, jnp.concatenate([fives[:, 1:], jnp.zeros((5, 1), samples.dtype)], axis=1),
         jnp.zeros((6, 16), samples.dtype)], axis=0)
    halo_windows = jnp.repeat(halo_windows, 16, axis=1)
    padded_first = jnp.concatenate([w_first, jnp.zeros((6, channels), w_first.dtype)])
    scratch = []
    for level in range(5):
        half = PHASES >> (level + 1)
        scratch.append(pltpu.VMEM((half + (level < 4), rows, channels), jnp.bfloat16))
        scratch.append(pltpu.VMEM((half, rows, channels), jnp.bfloat16))
    scratch += [pltpu.VMEM((2 * rows, channels), jnp.float32)] * 2
    return pl.pallas_call(
        encoder_kernel,
        out_shape=jax.ShapeDtypeStruct((rows + EXTRA, w_proj.shape[1]), jnp.bfloat16),
        in_specs=[pl.BlockSpec(memory_space=pltpu.VMEM)] * 7,
        out_specs=pl.BlockSpec(memory_space=pltpu.VMEM),
        scratch_shapes=scratch,
        compiler_params=pltpu.CompilerParams(vmem_limit_bytes=48 * 2**20),
        cost_estimate=pl.CostEstimate(flops=14 * 10**9, bytes_accessed=12 * 10**6, transcendentals=9 * 10**6),
        name="encoder",
    )(windows, halo_windows, padded_first, w_mid.reshape(4, 3, channels, channels),
      w_tail.reshape(2, 2, channels, channels), w_proj, extra)


def remote(source, target, sent, received, device):
    return pltpu.make_async_remote_copy(
        src_ref=source, dst_ref=target, send_sem=sent, recv_sem=received,
        device_id=device, device_id_type=pl.DeviceIdType.MESH,
    )


def gather_kernel(
    lines, cut, block, centroids, sums, counts, term, out, rounded, squares, terms, landed,
    own_sem, zs, zr, xs, xr, ys, yr, cs, cr, ts, tr,
):
    g, t = lax.axis_index("grp"), lax.axis_index("tm")
    h, c = lax.div(g, 2), lax.rem(g, 2)
    own, p = lax.div(t, 2), lax.rem(t, 2)
    rows = block.shape[0]
    over_p, over_h, over_c = (g, 2 * own + 1 - p), (2 * (1 - h) + c, t), (2 * h + 1 - c, t)
    above, below = own < lines - 1, own > 0
    barrier = pltpu.get_barrier_semaphore()
    devices = 2 * lines
    peers = [(g, lax.rem(t + step, devices)) for step in range(1, devices)]
    for device in peers + [over_h, over_c]:
        pl.semaphore_signal(barrier, inc=1, device_id=device, device_id_type=pl.DeviceIdType.MESH)
    pl.semaphore_wait(barrier, devices + 1)

    def slot(dh, dc, line, dp):
        hh = h if dh == 0 else 1 - h
        cc = c if dc == 0 else 1 - c
        pp = p if dp == 0 else 1 - p
        return out.at[2 * hh + cc, 2 * line + pp]

    def half(ref, which):
        return ref.at[pl.ds(0, cut), :] if which == 0 else ref.at[pl.ds(cut, rows - cut), :]

    def along(way, line, source=None):
        target = slot(0, 0, line, 0)
        return remote(target if source is None else source, target, zs.at[way, line], zr.at[line],
                      (g, t + 2 - 4 * way))

    def to_p(kind, line, source=None):
        target = slot(0, 0, line, 0) if kind == 0 else half(slot(1, 0, line, 0), 1)
        return remote(target if source is None else source, target, xs.at[kind, line], xr.at[kind, line], over_p)

    def to_h(kind, line, source=None):
        target = slot(0, 0, line, 0) if kind == 0 else half(slot(0, 0, line, 1), 0)
        return remote(target if source is None else source, target, ys.at[kind, line], yr.at[kind, line], over_h)

    def to_c(dh, dp, line, source=None):
        target = slot(dh, 0, line, dp)
        kind = 2 * dh + dp
        return remote(target if source is None else source, target, cs.at[kind, line], cr.at[kind, line], over_c)

    def arrived(target, sent, received):
        remote(target, target, sent, received, over_c).wait_recv()

    here = pltpu.make_async_copy(block, slot(0, 0, own, 0), own_sem)
    onward = (above, below)

    def spread(line, source=None):
        to_p(0, line, source).start()
        to_h(0, line, source).start()
        to_c(0, 0, line, source).start()

    for way in range(2):
        @pl.when(onward[way])
        def _(way=way):
            along(way, own, block).start()
    spread(own, block)
    here.start()

    def each(step, action):
        if step == 0:
            action(own, 0)
            return
        for way in range(2):
            line = own - step if way == 0 else own + step

            @pl.when((line >= 0) & (line < lines))
            def _(line=line, way=way):
                action(line, way)

    def first_visit(line, way):
        arrived(slot(0, 0, line, 0), zs.at[way, line], zr.at[line])

        @pl.when(onward[way])
        def _():
            along(way, line).start()

        spread(line)

    def second_visit(line, way):
        arrived(slot(0, 0, line, 1), xs.at[0, line], xr.at[0, line])
        to_h(1, line).start()
        to_c(0, 1, line).start()
        arrived(slot(1, 0, line, 0), ys.at[0, line], yr.at[0, line])
        to_p(1, line).start()
        to_c(1, 0, line).start()

    def third_visit(line, way):
        arrived(half(slot(1, 0, line, 1), 0), ys.at[1, line], yr.at[1, line])
        arrived(half(slot(1, 0, line, 1), 1), xs.at[1, line], xr.at[1, line])
        to_c(1, 1, line).start()

    shard, width = centroids.shape
    frame_rows = counts.shape[1]
    tile = min(512, shard)
    first_id = t * shard

    def prepare(i, carry):
        held = pl.ds(pl.multiple_of(i * tile, tile), tile)
        short = centroids[held, :].astype(jnp.bfloat16)
        rounded[held, :] = short
        wide = short.astype(jnp.float32)
        squares[held, :] = jnp.broadcast_to(jnp.sum(wide * wide, axis=1, keepdims=True), (tile, frame_rows))
        sums[held, :] = jnp.zeros((tile, width), jnp.float32)
        counts[held, :] = jnp.zeros((tile, frame_rows), jnp.float32)
        return carry

    lax.fori_loop(0, shard // tile, prepare, 0)

    def accumulate(dh, dc, line, scored):
        group = 2 * (h if dh == 0 else 1 - h) + (c if dc == 0 else 1 - c)
        pair = [out[group, 2 * line + k, pl.ds(0, frame_rows), :] for k in range(2)]
        pair = jnp.concatenate(pair, axis=0)
        labels = []
        for k in range(2):
            digits = out[group, 2 * line + k, pl.ds(frame_rows, EXTRA), pl.ds(0, frame_rows)].astype(jnp.float32)
            labels.append(digits[0:1] * float(RADIX) + digits[1:2])
        labels = jnp.concatenate(labels, axis=1)

        def one(i, picked):
            held = pl.ds(pl.multiple_of(i * tile, tile), tile)
            ids = lax.broadcasted_iota(jnp.int32, (tile, 2 * frame_rows), 0) + (first_id + i * tile)
            hot = ids.astype(jnp.float32) == labels
            ones = jnp.where(hot, 1.0, 0.0)
            sums[held, :] += dot(ones.astype(jnp.bfloat16), pair)
            counts[held, :] += ones[:, :frame_rows] + ones[:, frame_rows:]
            if not scored:
                return picked
            products = lax.dot_general(
                rounded[held, :], pair, (((1,), (1,)), ((), ())), preferred_element_type=jnp.float32
            )
            value = jnp.where(hot, squares[held, :][:, :1] - 2.0 * products, 0.0)
            return picked + jnp.sum(value, axis=0, keepdims=True)

        picked = lax.fori_loop(0, shard // tile, one, jnp.zeros((1, 2 * frame_rows), jnp.float32))
        if scored:
            terms[2 * line] = picked[:, :frame_rows]
            terms[2 * line + 1] = picked[:, frame_rows:]

    def each_rolled(step, action):
        if step < 0 or step >= lines:
            return
        if step == 0:
            action(own)
            return

        def body(way, carry):
            line = own - step + 2 * step * way

            @pl.when((line >= 0) & (line < lines))
            def _():
                action(line)

            return carry

        lax.fori_loop(0, 2, body, 0)

    def to_peer(peer):
        return remote(terms.at[peer], landed.at[t], ts.at[peer], tr.at[t], (g, peer))

    def compute_0(line):
        accumulate(0, 0, line, True)

    def compute_1(line):
        for dp in range(2):
            arrived(slot(0, 1, line, dp), cs.at[dp, line], cr.at[dp, line])
        for k in range(2):
            @pl.when(2 * line + k != t)
            def _(k=k):
                to_peer(2 * line + k).start()

        accumulate(0, 1, line, False)

    def compute_2(line):
        accumulate(1, 0, line, False)

    def compute_3(line):
        for dp in range(2):
            arrived(slot(1, 1, line, dp), cs.at[2 + dp, line], cr.at[2 + dp, line])
        accumulate(1, 1, line, False)

    for step in range(1, lines):
        each(step, first_visit)
        each(step - 1, second_visit)
        if step == 1:
            here.wait()
        each_rolled(step - 1, compute_0)
        each_rolled(step - 2, compute_1)
    each(lines - 1, second_visit)
    each_rolled(lines - 1, compute_0)
    each(0, third_visit)
    each_rolled(lines - 2, compute_1)
    for step in range(lines):
        if step + 1 < lines:
            each(step + 1, third_visit)
        each_rolled(step, compute_2)
        if step == 0:
            each_rolled(lines - 1, compute_1)
        each_rolled(step - 1, compute_3)
    each_rolled(lines - 1, compute_3)

    def last_visit(line, way):
        for dh in range(2):
            for dp in range(2):
                kind = 2 * dh + dp
                to_c(dh, dp, line).wait_send()
        for kind in range(2):
            to_p(kind, line).wait_send()
            to_h(kind, line).wait_send()

    for step in range(lines):
        each(step, last_visit)
    for step in range(1, lines):
        def sent_on(line, way):
            @pl.when(onward[way])
            def _():
                along(way, line).wait_send()

        each(step, sent_on)
    for way in range(2):
        @pl.when(onward[way])
        def _(way=way):
            along(way, own).wait_send()
    landed[t] = terms[t]

    def settle(peer, carry):
        @pl.when(peer != t)
        def _():
            to_peer(peer).wait_send()
            arrived_term = remote(landed.at[peer], landed.at[peer], ts.at[peer], tr.at[peer], over_c)
            arrived_term.wait_recv()

        return carry

    lax.fori_loop(0, devices, settle, 0)
    total = landed[0]
    for peer in range(1, devices):
        total = total + landed[peer]
    term[...] = total


def gather_and_sum(block, centroids, groups, count, frame_rows):
    lines = count // 2
    shard, width = centroids.shape
    dma = pltpu.SemaphoreType.DMA
    vmem = pl.BlockSpec(memory_space=pltpu.VMEM)
    return pl.pallas_call(
        lambda *refs: gather_kernel(lines, 64, *refs),
        out_shape=(
            jax.ShapeDtypeStruct((shard, width), jnp.float32),
            jax.ShapeDtypeStruct((shard, frame_rows), jnp.float32),
            jax.ShapeDtypeStruct((1, frame_rows), jnp.float32),
        ),
        in_specs=[vmem, vmem],
        out_specs=(vmem, vmem, vmem),
        scratch_shapes=[
            pltpu.VMEM((groups, count) + block.shape, block.dtype),
            pltpu.VMEM((shard, width), jnp.bfloat16),
            pltpu.VMEM((shard, frame_rows), jnp.float32),
            pltpu.VMEM((count, 1, frame_rows), jnp.float32),
            pltpu.VMEM((count, 1, frame_rows), jnp.float32),
            dma, dma((2, lines)), dma((lines,)), dma((2, lines)), dma((2, lines)),
            dma((2, lines)), dma((2, lines)), dma((4, lines)), dma((4, lines)),
            dma((count,)), dma((count,)),
        ],
        compiler_params=pltpu.CompilerParams(collective_id=0, has_side_effects=True, vmem_limit_bytes=50 * 2**20),
        name="gather_and_sum",
    )(block, centroids)


def local(wave, assign, w_first, w_mid, w_tail, w_proj, centroids, prior):
    samples = wave[0]
    tail_part = passed_along(samples[:HALO], "tm", -1)
    groups, count = lax.axis_size("grp"), lax.axis_size("tm")
    own_rows = assign.shape[1]
    feat_width = centroids.shape[1]
    digits = jnp.concatenate([assign // RADIX, assign % RADIX]).astype(jnp.bfloat16)
    extra = jnp.pad(digits, ((0, EXTRA - 2), (0, feat_width - own_rows)))
    block = encode(samples, tail_part, w_first, w_mid, w_tail, w_proj, extra)
    total_sums, lane_counts, term = gather_and_sum(block, centroids, groups, count, own_rows)
    own_frames = block[:own_rows].astype(jnp.float32)
    squares = jnp.sum(own_frames * own_frames, axis=1)
    distortion = (squares[None, :] + term) / feat_width
    total_counts = jnp.sum(lane_counts, axis=1)
    new_counts = prior + total_counts
    new_centroids = (prior[:, None] * centroids + total_sums) / new_counts[:, None]
    return (new_centroids, new_counts, distortion)


def solution(mesh):
    return jax.shard_map(
        local,
        mesh=mesh,
        in_specs=(P("grp", "tm"), P("grp", "tm"), P(), P(), P(), P(), P("tm", None), P("tm")),
        out_specs=(P("tm", None), P("tm"), P("grp", "tm")),
        check_vma=False,
    )
```
